32 devices in a mesh: rep: 2 (over y), grp: 8 (over z, x), sub: 2 (over core).
Axes of the slice: x: 2, y: 2, z: 4, core: 2. Of those that a mesh axis runs over, the one named last changes fastest.
Arguments:
- query_rows: bfloat16 [16, 4, 5120], P(('grp', 'sub'), 'rep'), parts along dimension 1, may hold values from -120 to 120
- cache_keys: bfloat16 [16, 4, 128, 1024], P(('grp', 'sub'), 'rep'), parts along dimension 1, may hold values from -6 to 6
- cache_values: bfloat16 [16, 4, 128, 1024], P(('grp', 'sub'), 'rep'), parts along dimension 1, may hold values from -6 to 6
- residual: bfloat16 [16, 4, 5120], P(('grp', 'sub'), 'rep'), parts along dimension 1, may hold values from -6 to 6
- lengths: int32 [16, 4], P(('grp', 'sub'), 'rep'), parts along dimension 1, may hold values from 3 to 128
- expert_ids: int32 [16, 4, 1], P(('grp', 'sub'), 'rep'), parts along dimension 1, may hold values from 0 to 3; in each aligned block of 2 rows (0 to 1, 2 to 3, ..., all dimensions but the last counted through in order) at most 2 rows name the same one
- capacity: int32 [4], replicated, may hold values from 1 to 2
- norm_gain: float32 [5120], replicated, may hold values from 0.5 to 1.5
- router: bfloat16 [5120, 4], replicated, may hold values from -0.078125 to 0.078125
- shared_gate: bfloat16 [5120, 8192], P(None, ('grp', 'sub')), may hold values from -0.078125 to 0.078125
- shared_up: bfloat16 [5120, 8192], P(None, ('grp', 'sub')), may hold values from -0.078125 to 0.078125
- shared_down: bfloat16 [8192, 5120], P(('grp', 'sub')), may hold values from -0.0625 to 0.0625
- expert_gate: bfloat16 [5120, 32768], P(None, ('grp', 'sub')), may hold values from -0.078125 to 0.078125
- expert_up: bfloat16 [5120, 32768], P(None, ('grp', 'sub')), may hold values from -0.078125 to 0.078125
- expert_down: bfloat16 [32768, 5120], P(('grp', 'sub')), may hold values from -0.0625 to 0.0625
Outputs:
- layer_out: bfloat16 [16, 4, 5120], P(('grp', 'sub'), 'rep'), parts along dimension 1
The draws below stay inside these ranges and needn't reach their ends.
There are 2 independent parts, one for each index of `rep`. The reference program is written for one: setup_inputs(seed, part) draws one part's arguments, and reference() takes and returns one part's arrays. A program takes and returns all parts, laid end to end along the dimension named above; an argument that names none is the same for every part. Nothing has to cross between parts.
Inputs may be any that keep to these rules, and one draw needn't show every extreme that they name: `expert_ids`: in each aligned block of 2 rows (the rows of one device), no expert is named more than 2 times.
All inputs are finite; a program needn't handle non-finite values.
Results may differ from the reference program's by a relative error of at most 0.0075.
Values may be sent and summed in bfloat16 or wider, within the bound.
No kernel may reach another device: no remote copies, remote signals or barrier semaphores. Data moves between devices by JAX's collectives and lax.ppermute only.
A program may use at most 128 MiB of HBM per device.

```python
import math
import jax
import jax.numpy as jnp
import numpy as np
from jax import lax

D = 5120
HEADS = 40
KV_HEADS = 8
HEAD = 128
EXPERTS = 4
EH = 8192
SH = 8192
CTX = 128
REQ_DEV = 2
HOLDERS = 16
CAP = 2


def query_key_pair(key):
    base_key = jax.random.fold_in(key, 91)
    key_part = jnp.clip(jax.random.normal(jax.random.fold_in(base_key, 1), (HOLDERS, REQ_DEV, CTX, KV_HEADS * HEAD), jnp.float32), -6.0, 6.0)
    query_part = jnp.clip(jax.random.normal(jax.random.fold_in(base_key, 2), (HOLDERS, REQ_DEV, HEADS * HEAD), jnp.float32), -6.0, 6.0)
    return (query_part, key_part)


def draw_query_rows(key, part):
    query_part, key_part = query_key_pair(key)
    return query_part.astype(jnp.bfloat16)


def draw_cache_keys(key, part):
    query_part, key_part = query_key_pair(key)
    return key_part.astype(jnp.bfloat16)


def plant(values, key, low, largest):
    spot = [jax.random.randint(jax.random.fold_in(key, axis), (), 0, length) for axis, length in enumerate(values.shape)]
    longest = values.shape.index(max(values.shape))
    beside = spot[:longest] + [(spot[longest] + 1) % values.shape[longest]] + spot[longest + 1:]
    return values.at[tuple(spot)].set(low).at[tuple(beside)].set(largest)


def shard_levels(key, shape, split, least, high):
    def one(dim, shards_of):
        steps = jax.random.uniform(jax.random.fold_in(jax.random.fold_in(key, 6), dim), (shards_of,), jnp.float32, least / len(split), high / len(split))
        return jnp.repeat(jnp.exp(steps), shape[dim] // shards_of).reshape((-1,) + (1,) * (len(shape) - dim - 1))

    factor_of = one(*split[0])
    for cut in split[1:]:
        factor_of = factor_of * one(*cut)
    return factor_of


def deal_out(key, own, number, rows, count, top, limit, slope):
    order = jax.random.permutation(key, count)
    heavy_load, ordinary = portions_of(count, rows * top, limit, slope, True), portions_of(count, rows * top, limit, slope, False)
    places = jnp.arange(count)

    def named(sizes, rotation):
        used = int((sizes > 0).sum())
        fixed = max(1, used // 4)
        moved = fixed + (places - fixed + rotation * (used - fixed)) % max(1, count - fixed)
        return jnp.zeros((count,), jnp.int32).at[order[jnp.where(places < fixed, places, moved)]].set(jnp.asarray(sizes, jnp.int32))

    sizes = jnp.where(number % 4 == 0, named(heavy_load, number // 4), named(ordinary, number - number // 4 - 1))
    mixed = jax.random.permutation(jax.random.fold_in(own, 3), count)
    giver, sink = mixed[0:count // 2 * 2:2], mixed[1:count // 2 * 2:2]
    margin = jnp.minimum(sizes[giver] - 1, limit - sizes[sink]) // 2
    margin = jnp.where((giver == order[0]) | (sink == order[0]) | (sizes[sink] == 0), 0, jnp.maximum(margin, 0))
    moved = jax.random.randint(jax.random.fold_in(own, 4), (count // 2,), 0, 1 << 20) % (margin + 1)
    sizes = sizes.at[giver].add(-moved).at[sink].add(moved)
    labels = jnp.searchsorted(jnp.cumsum(sizes), jnp.arange(rows * top), side="right").astype(jnp.int32)
    grid = labels.reshape(top, rows).T
    grid = grid[jax.random.permutation(jax.random.fold_in(own, 1), rows)]
    rotation = jax.random.randint(jax.random.fold_in(own, 2), (rows, 1), 0, top)
    return jnp.take_along_axis(grid, (jnp.arange(top)[None, :] + rotation) % top, axis=1)


def portions_of(number_of, total, reach, skew, full):
    portions = [(1 << 20) // math.isqrt(standing ** skew) + 1 for standing in range(1, number_of + 1)]
    largest = reach if full else min(reach, max(-(-total // number_of), total * portions[0] // sum(portions)))
    least = 1 if total - largest >= number_of - 1 else 0
    counts, surplus = [largest] + [least] * (number_of - 1), total - largest - least * (number_of - 1)
    while surplus > 0:
        free = [i for i in range(1, number_of) if counts[i] < largest] or [i for i in range(1, number_of) if counts[i] < reach]
        pool, budget = sum([portions[i] for i in free]), surplus
        for i in free:
            addition = min(reach - counts[i], max(1, budget * portions[i] // pool), surplus)
            counts[i] = counts[i] + addition
            surplus = surplus - addition
    return np.array(counts)


def centred(key, extent, deviation, reach, cuts=(), kind=jnp.bfloat16):
    drawn = jax.random.normal(key, extent, jnp.float32) * deviation
    if len(cuts) > 0:
        drawn = shard_levels(key, extent, cuts, -0.22, 0.18) * drawn
    return jnp.clip(drawn, min=-reach, max=reach).astype(kind)


def setup_inputs(seed: int = 0, part: int = 0) -> dict:
    keys = jax.random.split(jax.random.key(seed), 16)
    part_splits = jax.random.split(jax.random.fold_in(keys[15], part), 16)
    query_rows = draw_query_rows(jax.random.fold_in(jax.random.fold_in(keys[15], part), 71), part)
    cache_keys = draw_cache_keys(jax.random.fold_in(jax.random.fold_in(keys[15], part), 71), part)
    cache_values = centred(part_splits[2], (HOLDERS, REQ_DEV, CTX, KV_HEADS * HEAD), 1.0, 6.0, ((0, 16),))
    residual = centred(part_splits[3], (HOLDERS, REQ_DEV, D), 1.0, 6.0, ((0, 16),))
    lengths = plant(jax.random.randint(part_splits[4], (HOLDERS, REQ_DEV), 3, CTX + 1), jax.random.fold_in(part_splits[4], 1), 3, CTX).astype(jnp.int32)
    expert_ids_keys = jax.random.split(jax.random.fold_in(part_splits[5], 1), HOLDERS * REQ_DEV // REQ_DEV)
    expert_ids_turns = jax.random.permutation(jax.random.fold_in(part_splits[5], 3), HOLDERS * REQ_DEV // REQ_DEV)
    expert_ids = jax.vmap(lambda own, number: deal_out(jax.random.fold_in(part_splits[5], 2), own, number, REQ_DEV, EXPERTS, 1, CAP, 2))(expert_ids_keys, expert_ids_turns).reshape((HOLDERS, REQ_DEV, 1))
    capacity = plant(jax.random.randint(keys[6], (EXPERTS,), max(1, CAP // 2), CAP + 1), jax.random.fold_in(keys[6], 1), max(1, CAP // 2), CAP).astype(jnp.int32)
    norm_gain = jnp.clip(1.0 + 0.1 * jax.random.normal(keys[7], (D,), jnp.float32), 0.5, 1.5)
    router = centred(keys[8], (D, EXPERTS), D ** -0.5, 0.078125)
    shared_gate = centred(keys[9], (D, SH), D ** -0.5, 0.078125, ((1, 16),))
    shared_up = centred(keys[10], (D, SH), D ** -0.5, 0.078125, ((1, 16),))
    shared_down = centred(keys[11], (SH, D), SH ** -0.5, 0.0625, ((0, 16),))
    expert_gate = centred(keys[12], (D, EXPERTS * EH), D ** -0.5, 0.078125, ((1, 16),))
    expert_up = centred(keys[13], (D, EXPERTS * EH), D ** -0.5, 0.078125, ((1, 16),))
    expert_down = centred(keys[14], (EXPERTS * EH, D), EH ** -0.5, 0.0625, ((0, 16),))
    return dict(query_rows=query_rows, cache_keys=cache_keys, cache_values=cache_values, residual=residual, lengths=lengths, expert_ids=expert_ids, capacity=capacity, norm_gain=norm_gain, router=router, shared_gate=shared_gate, shared_up=shared_up, shared_down=shared_down, expert_gate=expert_gate, expert_up=expert_up, expert_down=expert_down)


def attend(query_rows, cache_keys, cache_values, lengths):
    request_count = query_rows.shape[0]
    groups = HEADS // KV_HEADS
    queries_f = query_rows.astype(jnp.float32).reshape(request_count, KV_HEADS, groups, HEAD)
    keys_f = cache_keys.astype(jnp.float32).reshape(request_count, CTX, KV_HEADS, HEAD)
    scores = jnp.einsum('rkgh,rjkh->rkgj', queries_f, keys_f) * HEAD ** (-0.5)
    key_pos = jnp.arange(CTX, dtype=jnp.int32)
    allowed = (key_pos[None, :] < lengths[:, None])[:, None, None, :]
    scores = jnp.where(allowed, scores, -1e+30)
    row_peak = lax.optimization_barrier(jnp.max(scores, axis=-1, keepdims=True))
    exponent = jnp.where(allowed, jnp.exp(scores - row_peak), 0.0)
    weights = (exponent / lax.optimization_barrier(jnp.sum(exponent, axis=-1, keepdims=True))).astype(jnp.bfloat16)
    values_f = cache_values.astype(jnp.float32).reshape(request_count, CTX, KV_HEADS, HEAD)
    attended = jnp.einsum('rkgj,rjkh->rkgh', weights.astype(jnp.float32), values_f)
    return attended.reshape(request_count, HEADS * HEAD).astype(jnp.bfloat16)

def rms_normalize(stream, norm_gain):
    mean_square = lax.optimization_barrier(jnp.mean(stream * stream, axis=-1, keepdims=True))
    return (stream * lax.rsqrt(mean_square + 1e-05) * norm_gain).astype(jnp.bfloat16)

def swiglu(inputs, w_gate, w_up, w_down):
    gate_part = jnp.dot(inputs, w_gate, preferred_element_type=jnp.float32)
    up_part = jnp.dot(inputs, w_up, preferred_element_type=jnp.float32)
    hidden = (jax.nn.silu(gate_part) * up_part).astype(jnp.bfloat16)
    return jnp.dot(hidden, w_down, preferred_element_type=jnp.float32)

def gated_inputs(flat_rows, router, route_ids):
    logits = jnp.dot(flat_rows, router, preferred_element_type=jnp.float32)
    onehot = route_ids[:, None] == jnp.arange(EXPERTS, dtype=jnp.int32)[None, :]
    picked = lax.optimization_barrier(jnp.sum(jnp.where(onehot, logits, 0.0), axis=-1))
    return (flat_rows.astype(jnp.float32) * jax.nn.sigmoid(picked)[:, None]).astype(jnp.bfloat16)

def build_slots(route_ids, capacity):
    onehot = (route_ids[:, None] == jnp.arange(EXPERTS, dtype=jnp.int32)[None, :]).astype(jnp.int32)
    before = jnp.cumsum(onehot, axis=0) - onehot
    row_rank = lax.optimization_barrier(jnp.sum(before * onehot, axis=1))
    row_limit = lax.optimization_barrier(jnp.sum(onehot * capacity[None, :], axis=1))
    kept_rows = row_rank < row_limit
    expert_match = route_ids[None, None, :] == jnp.arange(EXPERTS, dtype=jnp.int32)[:, None, None]
    slot_match = row_rank[None, None, :] == jnp.arange(CAP, dtype=jnp.int32)[None, :, None]
    return (expert_match & slot_match & kept_rows[None, None, :]).astype(jnp.float32)

def reference(query_rows, cache_keys, cache_values, residual, lengths, expert_ids, capacity, norm_gain, router, shared_gate, shared_up, shared_down, expert_gate, expert_up, expert_down):
    row_count = HOLDERS * REQ_DEV
    attended = attend(query_rows.reshape(row_count, HEADS * HEAD), cache_keys.reshape(row_count, CTX, KV_HEADS * HEAD), cache_values.reshape(row_count, CTX, KV_HEADS * HEAD), lengths.reshape(row_count))
    stream = residual.reshape(row_count, D).astype(jnp.float32) + attended.astype(jnp.float32)
    flat_rows = rms_normalize(stream, norm_gain)
    shared_out = swiglu(flat_rows, shared_gate, shared_up, shared_down)
    route_ids = expert_ids.reshape(row_count)
    scaled = gated_inputs(flat_rows, router, route_ids)
    blocks = HOLDERS
    selection = jax.vmap(build_slots, in_axes=(0, None))(route_ids.reshape(blocks, REQ_DEV), capacity)
    slot_rows = jnp.einsum('becr,brd->ebcd', selection, scaled.reshape(blocks, REQ_DEV, D).astype(jnp.float32))
    slot_rows = slot_rows.astype(jnp.bfloat16).reshape(EXPERTS, blocks * CAP, D)

    def one_expert(packed):
        expert_index, inputs = packed
        start_col = expert_index * EH
        w_gate = lax.dynamic_slice_in_dim(expert_gate, start_col, EH, 1)
        w_up = lax.dynamic_slice_in_dim(expert_up, start_col, EH, 1)
        w_down = lax.dynamic_slice_in_dim(expert_down, start_col, EH, 0)
        return swiglu(inputs, w_gate, w_up, w_down)
    expert_out = lax.map(one_expert, (jnp.arange(EXPERTS, dtype=jnp.int32), slot_rows))
    routed = jnp.einsum('becr,ebcd->brd', selection, expert_out.reshape(EXPERTS, blocks, CAP, D))
    layer_out = stream + shared_out + routed.reshape(row_count, D)
    return layer_out.astype(jnp.bfloat16).reshape(HOLDERS, REQ_DEV, D)
```

```python
import functools
import jax
import jax.numpy as jnp
from jax import lax
from jax.experimental import pallas as pl
from jax.experimental.pallas import tpu as pltpu
from jax.sharding import PartitionSpec as P

HEADS = 40
KV_HEADS = 8
HEAD = 128
EXPERTS = 4
EXTRA = 128


def split3(v):
    parts = []
    for _ in range(3):
        part = v.astype(jnp.bfloat16)
        parts.append(part.astype(jnp.float32))
        v = v - parts[-1]
    return parts


def attend_kernel(len_hbm, ids_hbm, cap_hbm, q_hbm, k_hbm, v_hbm, res_hbm, gain_hbm, router_hbm,
                  row_ref, stream_ref,
                  len_ref, ids_ref, cap_ref, q_ref, k_ref, v_ref, res_ref, gain_ref, router_ref, sem):
    moves = ((q_hbm, q_ref), (k_hbm, k_ref), (len_hbm, len_ref), (v_hbm, v_ref), (res_hbm, res_ref), (gain_hbm, gain_ref),
             (router_hbm, router_ref), (ids_hbm, ids_ref), (cap_hbm, cap_ref))
    copies = [pltpu.make_async_copy(src, dst, sem.at[i]) for i, (src, dst) in enumerate(moves)]
    for copy in copies:
        copy.start()
    toks, context = k_ref.shape[0], k_ref.shape[1]
    groups = HEADS // KV_HEADS
    width = q_ref.shape[1]
    lane = lax.broadcasted_iota(jnp.int32, (1, EXTRA), 1)
    for copy in copies[:3]:
        copy.wait()
    scores = []
    for r in range(toks):
        queries = q_ref[r:r + 1, :].astype(jnp.float32)
        for h in range(KV_HEADS):
            base = h * groups * HEAD
            heads = [queries[:, base + g * HEAD:base + (g + 1) * HEAD] for g in range(groups)]
            heads += [jnp.zeros((8 - groups, HEAD), jnp.float32)]
            stacked = jnp.concatenate(heads, axis=0).astype(jnp.bfloat16)
            keys = k_ref[r, :, h * HEAD:(h + 1) * HEAD]
            scores.append(lax.dot_general(stacked, keys, (((1,), (1,)), ((), ())), preferred_element_type=jnp.float32))
    key_pos = lax.broadcasted_iota(jnp.int32, (8 * KV_HEADS, context), 1)
    allowed = jnp.concatenate([key_pos < len_ref[r] for r in range(toks)], axis=0)
    scores = jnp.where(allowed, jnp.concatenate(scores, axis=0) * HEAD ** (-0.5), -1e30)
    peak = jnp.max(scores, axis=-1, keepdims=True)
    expo = jnp.where(allowed, jnp.exp(scores - peak), 0.0)
    weights = (expo / jnp.sum(expo, axis=-1, keepdims=True)).astype(jnp.bfloat16).astype(jnp.float32)
    for copy in copies[3:]:
        copy.wait()
    attended = []
    for r in range(toks):
        for h in range(KV_HEADS):
            top = (r * KV_HEADS + h) * 8
            vals = v_ref[r, :, h * HEAD:(h + 1) * HEAD]
            attended.append(jnp.dot(weights[top:top + 8].astype(jnp.bfloat16), vals, preferred_element_type=jnp.float32))
    attended = [
        jnp.concatenate([attended[r * KV_HEADS + h][g:g + 1] for h in range(KV_HEADS) for g in range(groups)], axis=1)
        for r in range(toks)
    ]
    attended = jnp.concatenate(attended, axis=0).astype(jnp.bfloat16).astype(jnp.float32)
    stream = res_ref[...].astype(jnp.float32) + attended
    mean_square = jnp.mean(stream * stream, axis=-1, keepdims=True)
    normed = (stream * lax.rsqrt(mean_square + 1e-05) * gain_ref[...]).astype(jnp.bfloat16)
    stream_ref[...] = stream
    row_ref[:, :width] = normed
    values = normed.astype(jnp.float32)
    for r in range(toks):
        expert = ids_ref[r]
        column = jnp.zeros((1, width), jnp.float32)
        for e in range(EXPERTS):
            column = jnp.where(expert == e, router_ref[e:e + 1, :].astype(jnp.float32), column)
        logit = jnp.sum(values[r:r + 1] * column, axis=-1, keepdims=True)
        gate = 1.0 / (1.0 + jnp.exp(-logit))
        rank = jnp.int32(0)
        for s in range(r):
            rank = rank + (ids_ref[s] == expert).astype(jnp.int32)
        kept = rank < cap_ref[expert]
        label = jnp.where(kept, expert, -1).astype(jnp.float32)
        one, two, three = split3(gate)
        extra = jnp.where(lane == 0, label, jnp.where(lane == 1, one, jnp.where(lane == 2, two, jnp.where(lane == 3, three, 0.0))))
        row_ref[r:r + 1, width:] = extra.astype(jnp.bfloat16)


def ffn_kernel(bn, bd, per_slot, slots, front_ref, back_ref, own_ref, sg_hbm, su_hbm, sd_hbm, eg_hbm, eu_hbm, ed_hbm,
               keep_ref, send_ref, buf, ins_ref, sd_ref, normed, scaled, hidden, shared, sem, shared_sem):
    width = sg_hbm.shape[0]
    units = eu_hbm.shape[1]
    half = keep_ref.shape[0]
    ups = units // bn
    downs = width // (bd * per_slot)

    def columns(src, i):
        return lambda slot: [pltpu.make_async_copy(src.at[:, pl.ds(i * bn, bn)], buf.at[slot, pl.ds(0, width), pl.ds(0, bn)], sem.at[slot, 0])]

    def blocks(i):
        return lambda slot: [
            pltpu.make_async_copy(
                ed_hbm.at[:, pl.ds((i * per_slot + j) * bd, bd)],
                buf.at[slot, pl.ds(j * units, units), pl.ds(0, bd)],
                sem.at[slot, j],
            )
            for j in range(per_slot)
        ]

    loads = []
    for i in range(ups):
        loads += [columns(eg_hbm, i), columns(eu_hbm, i)]
    before_down = len(loads)
    shared_loads = [pltpu.make_async_copy(src, dst, shared_sem.at[i]) for i, (src, dst) in enumerate(
        ((sg_hbm, ins_ref.at[0]), (su_hbm, ins_ref.at[1]), (sd_hbm, sd_ref)))]
    loads += [blocks(i) for i in range(downs)]
    place = iter(range(len(loads)))

    def start(i):
        if i == before_down:
            shared_loads[2].start()
        if i < len(loads):
            for copy in loads[i](i % slots):
                copy.start()

    def arrive():
        i = next(place)
        for copy in loads[i](i % slots):
            copy.wait()
        return i, i % slots

    shared_loads[0].start()
    shared_loads[1].start()
    for i in range(slots):
        start(i)

    rows = front_ref.shape[0]
    for part, ref in enumerate((front_ref, back_ref)):
        values = ref[:, :width]
        extra = ref[:, width:].astype(jnp.float32)
        gate = extra[:, 1:2] + extra[:, 2:3] + extra[:, 3:4]
        gate = jnp.where(extra[:, 0:1] == own_ref[0].astype(jnp.float32), gate, 0.0)
        normed[part * rows:(part + 1) * rows] = values
        scaled[part * rows:(part + 1) * rows] = (values.astype(jnp.float32) * gate).astype(jnp.bfloat16)

    def swish(g, u):
        return (g / (1.0 + jnp.exp(-g)) * u).astype(jnp.bfloat16)

    def times(lhs, rhs):
        return jnp.dot(lhs, rhs, preferred_element_type=jnp.float32)

    def product():
        at, slot = arrive()
        out = times(scaled[...], buf[slot, :width, :bn])
        start(at + slots)
        return out

    shared_loads[0].wait()
    g = times(normed[...], ins_ref[0])
    shared_loads[1].wait()
    shared[...] = swish(g, times(normed[...], ins_ref[1]))
    for i in range(ups):
        g = product()
        hidden[:, i * bn:(i + 1) * bn] = swish(g, product())
    shared_loads[2].wait()
    for i in range(downs):
        at, slot = arrive()
        for j in range(per_slot):
            col = (i * per_slot + j) * bd
            out = times(shared[...], sd_ref[:, col:col + bd]) + times(hidden[...], buf[slot, j * units:(j + 1) * units, :bd])
            keep_ref[:, col:col + bd] = out[:half]
            send_ref[:, col:col + bd] = out[half:].astype(jnp.bfloat16)
        start(at + slots)


SMEM = pl.BlockSpec(memory_space=pltpu.SMEM)
VMEM = pl.BlockSpec(memory_space=pltpu.VMEM)
HBM = pl.BlockSpec(memory_space=pltpu.MemorySpace.HBM)


def afar(array):
    return pltpu.with_memory_space_constraint(array, pltpu.HBM)


def attend_rows(query_rows, cache_keys, cache_values, residual, lengths, ids, capacity, norm_gain, router):
    toks, width = query_rows.shape
    operands = (query_rows, cache_keys, cache_values, residual, norm_gain.reshape(1, width), router.T)
    return pl.pallas_call(
        attend_kernel,
        out_shape=(
            jax.ShapeDtypeStruct((toks, width + EXTRA), jnp.bfloat16),
            jax.ShapeDtypeStruct((toks, width), jnp.float32),
        ),
        in_specs=[HBM] * 9,
        out_specs=(VMEM, VMEM),
        scratch_shapes=[pltpu.SMEM(a.shape, a.dtype) for a in (lengths, ids, capacity)]
        + [pltpu.VMEM(a.shape, a.dtype) for a in operands]
        + [pltpu.SemaphoreType.DMA((9,))],
        cost_estimate=pl.CostEstimate(flops=0, bytes_accessed=1 << 20, transcendentals=0),
        compiler_params=pltpu.CompilerParams(vmem_limit_bytes=8 << 20),
        name="attend_rows",
    )(*map(afar, (lengths, ids, capacity, *operands)))


def feed_forward(front, back, own, shared_gate, shared_up, shared_down, expert_gate, expert_up, expert_down):
    count = 2 * front.shape[0]
    width, units = expert_gate.shape
    shared_units = shared_gate.shape[1]
    bn = min(512, units)
    bd = 512 if width % 512 == 0 else width
    assert units % bn == 0
    per_slot = max(q for q in range(1, width // bd + 1) if (width // bd) % q == 0 and (q == 1 or q * units <= width))
    slot_rows = max(width, per_slot * units)
    slots = 6
    half = count // 2
    weight_bytes = 2 * 3 * width * (units + shared_units)
    return pl.pallas_call(
        functools.partial(ffn_kernel, bn, bd, per_slot, slots),
        out_shape=(pltpu.VMEM((half, width), jnp.float32), pltpu.VMEM((half, width), jnp.bfloat16)),
        in_specs=[VMEM, VMEM, SMEM] + [HBM] * 6,
        out_specs=(VMEM, VMEM),
        scratch_shapes=[
            pltpu.VMEM((slots, slot_rows, max(bn, bd)), jnp.bfloat16),
            pltpu.VMEM((2, *shared_gate.shape), jnp.bfloat16),
            pltpu.VMEM(shared_down.shape, jnp.bfloat16),
            pltpu.VMEM((count, width), jnp.bfloat16),
            pltpu.VMEM((count, width), jnp.bfloat16),
            pltpu.VMEM((count, units), jnp.bfloat16),
            pltpu.VMEM((count, shared_units), jnp.bfloat16),
            pltpu.SemaphoreType.DMA((slots, per_slot)),
            pltpu.SemaphoreType.DMA((3,)),
        ],
        cost_estimate=pl.CostEstimate(flops=count * weight_bytes, bytes_accessed=weight_bytes, transcendentals=0),
        compiler_params=pltpu.CompilerParams(vmem_limit_bytes=52 << 20),
        name="feed_forward",
    )(front, back, own, *map(afar, (shared_gate, shared_up, shared_down, expert_gate, expert_up, expert_down)))


def per_device(
    steps,
    query_rows,
    cache_keys,
    cache_values,
    residual,
    lengths,
    expert_ids,
    capacity,
    norm_gain,
    router,
    shared_gate,
    shared_up,
    shared_down,
    expert_gate,
    expert_up,
    expert_down,
):
    toks = query_rows.shape[1]
    units = expert_gate.shape[1]
    row, stream = attend_rows(
        query_rows[0], cache_keys[0], cache_values[0], residual[0], lengths[0],
        expert_ids[0].reshape(toks), capacity, norm_gain, router,
    )
    rows = row
    for i, (axis, pairs) in enumerate(steps):
        other = lax.ppermute(rows, axis, pairs)
        if i < len(steps) - 1:
            rows = jnp.concatenate([rows, other], axis=0)
    devices = lax.axis_size(("grp", "sub"))
    own = lax.axis_index(("grp", "sub")) * units // (units * devices // EXPERTS)
    keep, send = feed_forward(
        rows, other, own.astype(jnp.int32).reshape(1), shared_gate, shared_up, shared_down, expert_gate, expert_up, expert_down
    )
    for i, (axis, pairs) in enumerate(reversed(steps)):
        total = keep + lax.ppermute(send, axis, pairs).astype(jnp.float32)
        half = total.shape[0] // 2
        if i < len(steps) - 1:
            keep, send = total[:half], total[half:].astype(jnp.bfloat16)
    return (stream + total).astype(jnp.bfloat16)[None]


def exchange_steps(mesh):
    steps = []
    for axis in ("grp", "sub"):
        size = mesh.shape[axis]
        assert size & (size - 1) == 0
        bit = size >> 1
        while bit:
            steps.append((axis, tuple((i, i ^ bit) for i in range(size))))
            bit >>= 1
    return tuple(steps)


def solution(mesh):
    placed = (
        P(("grp", "sub"), "rep", None),
        P(("grp", "sub"), "rep", None, None),
        P(("grp", "sub"), "rep", None, None),
        P(("grp", "sub"), "rep", None),
        P(("grp", "sub"), "rep"),
        P(("grp", "sub"), "rep", None),
        P(),
        P(),
        P(),
        P(None, ("grp", "sub")),
        P(None, ("grp", "sub")),
        P(("grp", "sub"), None),
        P(None, ("grp", "sub")),
        P(None, ("grp", "sub")),
        P(("grp", "sub"), None),
    )
    return jax.shard_map(
        functools.partial(per_device, exchange_steps(mesh)),
        mesh=mesh,
        in_specs=placed,
        out_specs=P(("grp", "sub"), "rep", None),
        check_vma=False,
    )
```

```python
import functools
import jax
import jax.numpy as jnp
from jax import lax
from jax.experimental import pallas as pl
from jax.experimental.pallas import tpu as pltpu
from jax.sharding import PartitionSpec as P


HEADS = 40
KV_HEADS = 8
HEAD = 128
EXPERTS = 4
EXTRA = 128
FETCHES = 4


def split3(v):
    parts = []
    for _ in range(3):
        part = v.astype(jnp.bfloat16)
        parts.append(part.astype(jnp.float32))
        v = v - parts[-1]
    return parts


def attend_kernel(len_hbm, ids_hbm, cap_hbm, q_hbm, k_hbm, v_hbm, res_hbm, gain_hbm, router_hbm, sg_hbm,
                  row_ref, stream_ref, sg_out,
                  len_ref, ids_ref, cap_ref, q_ref, k_ref, v_ref, res_ref, gain_ref, router_ref, sem):
    moves = ((q_hbm, q_ref), (k_hbm, k_ref), (len_hbm, len_ref), (v_hbm, v_ref), (res_hbm, res_ref), (gain_hbm, gain_ref),
             (router_hbm, router_ref), (ids_hbm, ids_ref), (cap_hbm, cap_ref), (sg_hbm, sg_out))
    copies = [pltpu.make_async_copy(src, dst, sem.at[i]) for i, (src, dst) in enumerate(moves)]
    for copy in copies:
        copy.start()
    toks, context = k_ref.shape[0], k_ref.shape[1]
    groups = HEADS // KV_HEADS
    width = q_ref.shape[1]
    lane = lax.broadcasted_iota(jnp.int32, (1, EXTRA), 1)
    for copy in copies[:3]:
        copy.wait()
    scores = []
    for r in range(toks):
        queries = q_ref[r:r + 1, :].astype(jnp.float32)
        for h in range(KV_HEADS):
            base = h * groups * HEAD
            heads = [queries[:, base + g * HEAD:base + (g + 1) * HEAD] for g in range(groups)]
            heads += [jnp.zeros((8 - groups, HEAD), jnp.float32)]
            stacked = jnp.concatenate(heads, axis=0).astype(jnp.bfloat16)
            keys = k_ref[r, :, h * HEAD:(h + 1) * HEAD]
            scores.append(lax.dot_general(stacked, keys, (((1,), (1,)), ((), ())), preferred_element_type=jnp.float32))
    key_pos = lax.broadcasted_iota(jnp.int32, (8 * KV_HEADS, context), 1)
    allowed = jnp.concatenate([key_pos < len_ref[r] for r in range(toks)], axis=0)
    scores = jnp.where(allowed, jnp.concatenate(scores, axis=0) * HEAD ** (-0.5), -1e30)
    peak = jnp.max(scores, axis=-1, keepdims=True)
    expo = jnp.where(allowed, jnp.exp(scores - peak), 0.0)
    weights = (expo / jnp.sum(expo, axis=-1, keepdims=True)).astype(jnp.bfloat16).astype(jnp.float32)
    for copy in copies[3:9]:
        copy.wait()
    attended = []
    for r in range(toks):
        for h in range(KV_HEADS):
            top = (r * KV_HEADS + h) * 8
            vals = v_ref[r, :, h * HEAD:(h + 1) * HEAD]
            attended.append(jnp.dot(weights[top:top + 8].astype(jnp.bfloat16), vals, preferred_element_type=jnp.float32))
    attended = [
        jnp.concatenate([attended[r * KV_HEADS + h][g:g + 1] for h in range(KV_HEADS) for g in range(groups)], axis=1)
        for r in range(toks)
    ]
    attended = jnp.concatenate(attended, axis=0).astype(jnp.bfloat16).astype(jnp.float32)
    stream = res_ref[...].astype(jnp.float32) + attended
    mean_square = jnp.mean(stream * stream, axis=-1, keepdims=True)
    normed = (stream * lax.rsqrt(mean_square + 1e-05) * gain_ref[...]).astype(jnp.bfloat16)
    stream_ref[...] = stream
    row_ref[:, :width] = normed
    values = normed.astype(jnp.float32)
    for r in range(toks):
        expert = ids_ref[r]
        column = jnp.zeros((1, width), jnp.float32)
        for e in range(EXPERTS):
            column = jnp.where(expert == e, router_ref[e:e + 1, :].astype(jnp.float32), column)
        logit = jnp.sum(values[r:r + 1] * column, axis=-1, keepdims=True)
        gate = 1.0 / (1.0 + jnp.exp(-logit))
        rank = jnp.int32(0)
        for s in range(r):
            rank = rank + (ids_ref[s] == expert).astype(jnp.int32)
        kept = rank < cap_ref[expert]
        label = jnp.where(kept, expert, -1).astype(jnp.float32)
        one, two, three = split3(gate)
        extra = jnp.where(lane == 0, label, jnp.where(lane == 1, one, jnp.where(lane == 2, two, jnp.where(lane == 3, three, 0.0))))
        row_ref[r:r + 1, width:] = extra.astype(jnp.bfloat16)
    for copy in copies[9:]:
        copy.wait()


def fetch_kernel(start, size, src_hbm, dst_ref, sem):
    source = src_hbm if size is None else src_hbm.at[:, pl.ds(start, size)]
    copy = pltpu.make_async_copy(source, dst_ref, sem)
    copy.start()
    copy.wait()


def ffn_kernel(bn, bd, per_slot, slots, near, front_ref, back_ref, sg_ref, sd_ref, *refs):
    eg_refs, refs = refs[:near], refs[near:]
    su_hbm, eg_hbm, eu_hbm, ed_hbm, keep_ref, send_ref, buf, su_ref, gates, normed, scaled, hidden, shared, sem, su_sem = refs
    width = sg_ref.shape[0]
    units = eu_hbm.shape[1]
    half = keep_ref.shape[0]
    ups = units // bn
    expert_units = units * lax.axis_size(("grp", "sub")) // EXPERTS
    own = (lax.axis_index("grp") * lax.axis_size("sub") + lax.axis_index("sub")) * units // expert_units
    downs = width // (bd * per_slot)

    def columns(src, i):
        return lambda slot: [pltpu.make_async_copy(src.at[:, pl.ds(i * bn, bn)], buf.at[slot, pl.ds(0, width), pl.ds(0, bn)], sem.at[slot, 0])]

    def blocks(i):
        return lambda slot: [
            pltpu.make_async_copy(
                ed_hbm.at[:, pl.ds((i * per_slot + j) * bd, bd)],
                buf.at[slot, pl.ds(j * units, units), pl.ds(0, bd)],
                sem.at[slot, j],
            )
            for j in range(per_slot)
        ]

    loads = []
    for i in range(ups):
        loads += [columns(eg_hbm, i)] if i >= near else []
        loads += [columns(eu_hbm, i)]
    loads += [blocks(i) for i in range(downs)]
    place = iter(range(len(loads)))

    def start(i):
        if i < len(loads):
            for copy in loads[i](i % slots):
                copy.start()

    def arrive():
        i = next(place)
        for copy in loads[i](i % slots):
            copy.wait()
        return i, i % slots

    shared_up = pltpu.make_async_copy(su_hbm, su_ref, su_sem)
    shared_up.start()
    for i in range(slots):
        start(i)

    rows = front_ref.shape[0]
    for part, ref in enumerate((front_ref, back_ref)):
        values = ref[:, :width]
        extra = ref[:, width:].astype(jnp.float32)
        gate = extra[:, 1:2] + extra[:, 2:3] + extra[:, 3:4]
        gate = jnp.where(extra[:, 0:1] == own.astype(jnp.float32), gate, 0.0)
        normed[part * rows:(part + 1) * rows] = values
        scaled[part * rows:(part + 1) * rows] = (values.astype(jnp.float32) * gate).astype(jnp.bfloat16)

    def swish(g, u):
        return (g / (1.0 + jnp.exp(-g)) * u).astype(jnp.bfloat16)

    def times(lhs, rhs):
        return jnp.dot(lhs, rhs, preferred_element_type=jnp.float32)

    g = times(normed[...], sg_ref[...])
    for i in range(near):
        gates[:, i * bn:(i + 1) * bn] = times(scaled[...], eg_refs[i][...])
    shared_up.wait()
    shared[...] = swish(g, times(normed[...], su_ref[...]))
    for i in range(ups):
        if i < near:
            g = gates[:, i * bn:(i + 1) * bn]
        else:
            at, slot = arrive()
            g = times(scaled[...], buf[slot, :width, :bn])
            start(at + slots)
        at, slot = arrive()
        u = times(scaled[...], buf[slot, :width, :bn])
        start(at + slots)
        hidden[:, i * bn:(i + 1) * bn] = swish(g, u)
    for i in range(downs):
        at, slot = arrive()
        for j in range(per_slot):
            col = (i * per_slot + j) * bd
            out = times(shared[...], sd_ref[:, col:col + bd]) + times(hidden[...], buf[slot, j * units:(j + 1) * units, :bd])
            keep_ref[:, col:col + bd] = out[:half]
            send_ref[:, col:col + bd] = out[half:].astype(jnp.bfloat16)
        start(at + slots)


VMEM = pl.BlockSpec(memory_space=pltpu.VMEM)
HBM = pl.BlockSpec(memory_space=pltpu.MemorySpace.HBM)


def nearby(array):
    return pltpu.with_memory_space_constraint(array, pltpu.VMEM)


def afar(array):
    return pltpu.with_memory_space_constraint(array, pltpu.HBM)


def attend_rows(query_rows, cache_keys, cache_values, residual, lengths, ids, capacity, norm_gain, router, shared_gate):
    toks, width = query_rows.shape
    operands = (query_rows, cache_keys, cache_values, residual, norm_gain.reshape(1, width), router.T)
    return pl.pallas_call(
        attend_kernel,
        out_shape=(
            jax.ShapeDtypeStruct((toks, width + EXTRA), jnp.bfloat16),
            jax.ShapeDtypeStruct((toks, width), jnp.float32),
            pltpu.VMEM(shared_gate.shape, shared_gate.dtype),
        ),
        in_specs=[HBM] * 10,
        out_specs=(VMEM,) * 3,
        scratch_shapes=[pltpu.SMEM(a.shape, a.dtype) for a in (lengths, ids, capacity)]
        + [pltpu.VMEM(a.shape, a.dtype) for a in operands]
        + [pltpu.SemaphoreType.DMA((10,))],
        cost_estimate=pl.CostEstimate(flops=0, bytes_accessed=12 << 20, transcendentals=0),
        compiler_params=pltpu.CompilerParams(vmem_limit_bytes=16 << 20),
        name="attend_rows",
    )(*map(afar, (lengths, ids, capacity, *operands, shared_gate)))


def fetch(array, start=0, size=None):
    shape = array.shape if size is None else (array.shape[0], size)
    return pl.pallas_call(
        functools.partial(fetch_kernel, start, size),
        out_shape=pltpu.VMEM(shape, array.dtype),
        in_specs=[HBM],
        out_specs=VMEM,
        scratch_shapes=[pltpu.SemaphoreType.DMA],
        cost_estimate=pl.CostEstimate(flops=0, bytes_accessed=2 * shape[0] * shape[1], transcendentals=0),
        compiler_params=pltpu.CompilerParams(vmem_limit_bytes=1 << 20),
        name="fetch",
    )(afar(array))


def feed_forward(front, back, shared_gate, shared_down, gates, shared_up, expert_gate, expert_up, expert_down, bn):
    count = 2 * front.shape[0]
    width, units = expert_gate.shape
    shared_units = shared_gate.shape[1]
    bd = 512 if width % 512 == 0 else width
    assert units % bn == 0
    per_slot = max(q for q in range(1, width // bd + 1) if (width // bd) % q == 0 and (q == 1 or q * units <= width))
    slot_rows = max(width, per_slot * units)
    slots = 4
    half = count // 2
    weight_bytes = 2 * 3 * width * (units + shared_units)
    return pl.pallas_call(
        functools.partial(ffn_kernel, bn, bd, per_slot, slots, len(gates)),
        out_shape=(pltpu.VMEM((half, width), jnp.float32), pltpu.VMEM((half, width), jnp.bfloat16)),
        in_specs=[VMEM, VMEM] + [VMEM] * (2 + len(gates)) + [HBM] * 4,
        out_specs=(VMEM, VMEM),
        scratch_shapes=[
            pltpu.VMEM((slots, slot_rows, max(bn, bd)), jnp.bfloat16),
            pltpu.VMEM(shared_up.shape, jnp.bfloat16),
            pltpu.VMEM((count, max(1, len(gates)) * bn), jnp.float32),
            pltpu.VMEM((count, width), jnp.bfloat16),
            pltpu.VMEM((count, width), jnp.bfloat16),
            pltpu.VMEM((count, units), jnp.bfloat16),
            pltpu.VMEM((count, shared_units), jnp.bfloat16),
            pltpu.SemaphoreType.DMA((slots, per_slot)),
            pltpu.SemaphoreType.DMA,
        ],
        cost_estimate=pl.CostEstimate(flops=count * weight_bytes, bytes_accessed=weight_bytes, transcendentals=0),
        compiler_params=pltpu.CompilerParams(vmem_limit_bytes=28 << 20),
        name="feed_forward",
    )(front, back, nearby(shared_gate), nearby(shared_down), *map(nearby, gates),
      *map(afar, (shared_up, expert_gate, expert_up, expert_down)))


def per_device(
    steps,
    fetches,
    query_rows,
    cache_keys,
    cache_values,
    residual,
    lengths,
    expert_ids,
    capacity,
    norm_gain,
    router,
    shared_gate,
    shared_up,
    shared_down,
    expert_gate,
    expert_up,
    expert_down,
):
    toks = query_rows.shape[1]
    units = expert_gate.shape[1]
    bn = min(512, units)
    row, stream, near_gate = attend_rows(
        query_rows[0], cache_keys[0], cache_values[0], residual[0], lengths[0],
        expert_ids[0].reshape(toks), capacity, norm_gain, router, shared_gate,
    )
    wanted = [(shared_down,)] + [(expert_gate, i * bn, bn) for i in range(units // bn)]
    near = []
    for i in range(min(fetches, len(wanted))):
        near.append(fetch(*wanted[i]))
    rows = row
    for i, (axis, pairs) in enumerate(steps):
        other = lax.ppermute(rows, axis, pairs)
        if i < len(steps) - 1:
            rows = jnp.concatenate([rows, other], axis=0)
    keep, send = feed_forward(
        rows, other, near_gate, near[0], near[1:],
        shared_up, expert_gate, expert_up, expert_down, bn,
    )
    for i, (axis, pairs) in enumerate(reversed(steps)):
        total = keep + lax.ppermute(send, axis, pairs).astype(jnp.float32)
        half = total.shape[0] // 2
        if i < len(steps) - 1:
            keep, send = total[:half], total[half:].astype(jnp.bfloat16)
    return (stream + total).astype(jnp.bfloat16)[None]


def exchange_steps(mesh):
    steps = []
    for axis in ("grp", "sub"):
        size = mesh.shape[axis]
        assert size & (size - 1) == 0
        bit = size >> 1
        while bit:
            steps.append((axis, tuple((i, i ^ bit) for i in range(size))))
            bit >>= 1
    return tuple(steps)


def solution(mesh):
    placed = (
        P(("grp", "sub"), "rep", None),
        P(("grp", "sub"), "rep", None, None),
        P(("grp", "sub"), "rep", None, None),
        P(("grp", "sub"), "rep", None),
        P(("grp", "sub"), "rep"),
        P(("grp", "sub"), "rep", None),
        P(),
        P(),
        P(),
        P(None, ("grp", "sub")),
        P(None, ("grp", "sub")),
        P(("grp", "sub"), None),
        P(None, ("grp", "sub")),
        P(None, ("grp", "sub")),
        P(("grp", "sub"), None),
    )
    steps = exchange_steps(mesh)
    fetches = min(FETCHES, len(steps))
    return jax.shard_map(
        functools.partial(per_device, steps, fetches),
        mesh=mesh,
        in_specs=placed,
        out_specs=P(("grp", "sub"), "rep", None),
        check_vma=False,
    )
```

```python
import functools
import jax
import jax.numpy as jnp
from jax import lax
from jax.experimental import pallas as pl
from jax.experimental.pallas import tpu as pltpu
from jax.sharding import PartitionSpec as P


HEADS = 40
KV_HEADS = 8
HEAD = 128
EXPERTS = 4
EXTRA = 128
FETCHES = 4


def split3(v):
    parts = []
    for _ in range(3):
        part = v.astype(jnp.bfloat16)
        parts.append(part.astype(jnp.float32))
        v = v - parts[-1]
    return parts


def attend_kernel(len_hbm, ids_hbm, cap_hbm, q_hbm, k_hbm, v_hbm, res_hbm, gain_hbm, router_hbm, sg_hbm,
                  row_ref, stream_ref, sg_out,
                  len_ref, ids_ref, cap_ref, q_ref, k_ref, v_ref, res_ref, gain_ref, router_ref, sem):
    moves = ((q_hbm, q_ref), (k_hbm, k_ref), (len_hbm, len_ref), (v_hbm, v_ref), (res_hbm, res_ref), (gain_hbm, gain_ref),
             (router_hbm, router_ref), (ids_hbm, ids_ref), (cap_hbm, cap_ref), (sg_hbm, sg_out))
    copies = [pltpu.make_async_copy(src, dst, sem.at[i]) for i, (src, dst) in enumerate(moves)]
    for copy in copies:
        copy.start()
    toks, context = k_ref.shape[0], k_ref.shape[1]
    groups = HEADS // KV_HEADS
    width = q_ref.shape[1]
    lane = lax.broadcasted_iota(jnp.int32, (1, EXTRA), 1)
    for copy in copies[:3]:
        copy.wait()
    scores = []
    for r in range(toks):
        queries = q_ref[r:r + 1, :].astype(jnp.float32)
        for h in range(KV_HEADS):
            base = h * groups * HEAD
            heads = [queries[:, base + g * HEAD:base + (g + 1) * HEAD] for g in range(groups)]
            heads += [jnp.zeros((8 - groups, HEAD), jnp.float32)]
            stacked = jnp.concatenate(heads, axis=0).astype(jnp.bfloat16)
            keys = k_ref[r, :, h * HEAD:(h + 1) * HEAD]
            scores.append(lax.dot_general(stacked, keys, (((1,), (1,)), ((), ())), preferred_element_type=jnp.float32))
    key_pos = lax.broadcasted_iota(jnp.int32, (8 * KV_HEADS, context), 1)
    allowed = jnp.concatenate([key_pos < len_ref[r] for r in range(toks)], axis=0)
    scores = jnp.where(allowed, jnp.concatenate(scores, axis=0) * HEAD ** (-0.5), -1e30)
    peak = jnp.max(scores, axis=-1, keepdims=True)
    expo = jnp.where(allowed, jnp.exp(scores - peak), 0.0)
    weights = (expo / jnp.sum(expo, axis=-1, keepdims=True)).astype(jnp.bfloat16).astype(jnp.float32)
    for copy in copies[3:9]:
        copy.wait()
    attended = []
    for r in range(toks):
        for h in range(KV_HEADS):
            top = (r * KV_HEADS + h) * 8
            vals = v_ref[r, :, h * HEAD:(h + 1) * HEAD]
            attended.append(jnp.dot(weights[top:top + 8].astype(jnp.bfloat16), vals, preferred_element_type=jnp.float32))
    attended = [
        jnp.concatenate([attended[r * KV_HEADS + h][g:g + 1] for h in range(KV_HEADS) for g in range(groups)], axis=1)
        for r in range(toks)
    ]
    attended = jnp.concatenate(attended, axis=0).astype(jnp.bfloat16).astype(jnp.float32)
    stream = res_ref[...].astype(jnp.float32) + attended
    mean_square = jnp.mean(stream * stream, axis=-1, keepdims=True)
    normed = (stream * lax.rsqrt(mean_square + 1e-05) * gain_ref[...]).astype(jnp.bfloat16)
    stream_ref[...] = stream
    row_ref[:, :width] = normed
    values = normed.astype(jnp.float32)
    for r in range(toks):
        expert = ids_ref[r]
        column = jnp.zeros((1, width), jnp.float32)
        for e in range(EXPERTS):
            column = jnp.where(expert == e, router_ref[e:e + 1, :].astype(jnp.float32), column)
        logit = jnp.sum(values[r:r + 1] * column, axis=-1, keepdims=True)
        gate = 1.0 / (1.0 + jnp.exp(-logit))
        rank = jnp.int32(0)
        for s in range(r):
            rank = rank + (ids_ref[s] == expert).astype(jnp.int32)
        kept = rank < cap_ref[expert]
        label = jnp.where(kept, expert, -1).astype(jnp.float32)
        one, two, three = split3(gate)
        extra = jnp.where(lane == 0, label, jnp.where(lane == 1, one, jnp.where(lane == 2, two, jnp.where(lane == 3, three, 0.0))))
        row_ref[r:r + 1, width:] = extra.astype(jnp.bfloat16)
    for copy in copies[9:]:
        copy.wait()


def fetch_kernel(start, size, src_hbm, dst_ref, sem):
    source = src_hbm if size is None else src_hbm.at[:, pl.ds(start, size)]
    copy = pltpu.make_async_copy(source, dst_ref, sem)
    copy.start()
    copy.wait()


def ffn_kernel(bn, bd, per_slot, slots, near, front_ref, back_ref, sg_ref, sd_ref, *refs):
    eg_refs, refs = refs[:near], refs[near:]
    su_hbm, eg_hbm, eu_hbm, ed_hbm, keep_ref, send_ref, buf, su_ref, gates, normed, scaled, hidden, shared, sem, su_sem = refs
    width = sg_ref.shape[0]
    units = eu_hbm.shape[1]
    half = keep_ref.shape[0]
    ups = units // bn
    expert_units = units * lax.axis_size(("grp", "sub")) // EXPERTS
    own = (lax.axis_index("grp") * lax.axis_size("sub") + lax.axis_index("sub")) * units // expert_units
    downs = width // (bd * per_slot)

    def columns(src, i):
        return lambda slot: [pltpu.make_async_copy(src.at[:, pl.ds(i * bn, bn)], buf.at[slot, pl.ds(0, width), pl.ds(0, bn)], sem.at[slot, 0])]

    def blocks(i):
        return lambda slot: [
            pltpu.make_async_copy(
                ed_hbm.at[:, pl.ds((i * per_slot + j) * bd, bd)],
                buf.at[slot, pl.ds(j * units, units), pl.ds(0, bd)],
                sem.at[slot, j],
            )
            for j in range(per_slot)
        ]

    loads = []
    for i in range(ups):
        loads += [columns(eg_hbm, i)] if i >= near else []
        loads += [columns(eu_hbm, i)]
    loads += [blocks(i) for i in range(downs)]
    place = iter(range(len(loads)))

    def start(i):
        if i < len(loads):
            for copy in loads[i](i % slots):
                copy.start()

    def arrive():
        i = next(place)
        for copy in loads[i](i % slots):
            copy.wait()
        return i, i % slots

    shared_up = pltpu.make_async_copy(su_hbm, su_ref, su_sem)
    shared_up.start()
    for i in range(slots):
        start(i)

    rows = front_ref.shape[0]
    for part, ref in enumerate((front_ref, back_ref)):
        values = ref[:, :width]
        extra = ref[:, width:].astype(jnp.float32)
        gate = extra[:, 1:2] + extra[:, 2:3] + extra[:, 3:4]
        gate = jnp.where(extra[:, 0:1] == own.astype(jnp.float32), gate, 0.0)
        normed[part * rows:(part + 1) * rows] = values
        scaled[part * rows:(part + 1) * rows] = (values.astype(jnp.float32) * gate).astype(jnp.bfloat16)

    def swish(g, u):
        return (g / (1.0 + jnp.exp(-g)) * u).astype(jnp.bfloat16)

    def times(lhs, rhs):
        return jnp.dot(lhs, rhs, preferred_element_type=jnp.float32)

    g = times(normed[...], sg_ref[...])
    for i in range(near):
        gates[:, i * bn:(i + 1) * bn] = times(scaled[...], eg_refs[i][...])
    shared_up.wait()
    shared[...] = swish(g, times(normed[...], su_ref[...]))
    for i in range(ups):
        if i < near:
            g = gates[:, i * bn:(i + 1) * bn]
        else:
            at, slot = arrive()
            g = times(scaled[...], buf[slot, :width, :bn])
            start(at + slots)
        at, slot = arrive()
        u = times(scaled[...], buf[slot, :width, :bn])
        start(at + slots)
        hidden[:, i * bn:(i + 1) * bn] = swish(g, u)
    for i in range(downs):
        at, slot = arrive()
        for j in range(per_slot):
            col = (i * per_slot + j) * bd
            out = times(shared[...], sd_ref[:, col:col + bd]) + times(hidden[...], buf[slot, j * units:(j + 1) * units, :bd])
            keep_ref[:, col:col + bd] = out[:half]
            send_ref[:, col:col + bd] = out[half:].astype(jnp.bfloat16)
        start(at + slots)


VMEM = pl.BlockSpec(memory_space=pltpu.VMEM)
HBM = pl.BlockSpec(memory_space=pltpu.MemorySpace.HBM)


def nearby(array):
    return pltpu.with_memory_space_constraint(array, pltpu.VMEM)


def afar(array):
    return pltpu.with_memory_space_constraint(array, pltpu.HBM)


def attend_rows(query_rows, cache_keys, cache_values, residual, lengths, ids, capacity, norm_gain, router, shared_gate):
    toks, width = query_rows.shape
    operands = (query_rows, cache_keys, cache_values, residual, norm_gain.reshape(1, width), router.T)
    return pl.pallas_call(
        attend_kernel,
        out_shape=(
            jax.ShapeDtypeStruct((toks, width + EXTRA), jnp.bfloat16),
            jax.ShapeDtypeStruct((toks, width), jnp.float32),
            pltpu.VMEM(shared_gate.shape, shared_gate.dtype),
        ),
        in_specs=[HBM] * 10,
        out_specs=(VMEM,) * 3,
        scratch_shapes=[pltpu.SMEM(a.shape, a.dtype) for a in (lengths, ids, capacity)]
        + [pltpu.VMEM(a.shape, a.dtype) for a in operands]
        + [pltpu.SemaphoreType.DMA((10,))],
        cost_estimate=pl.CostEstimate(flops=0, bytes_accessed=12 << 20, transcendentals=0),
        compiler_params=pltpu.CompilerParams(vmem_limit_bytes=16 << 20),
        name="attend_rows",
    )(*map(afar, (lengths, ids, capacity, *operands, shared_gate)))


def fetch(array, start=0, size=None):
    shape = array.shape if size is None else (array.shape[0], size)
    return pl.pallas_call(
        functools.partial(fetch_kernel, start, size),
        out_shape=pltpu.VMEM(shape, array.dtype),
        in_specs=[HBM],
        out_specs=VMEM,
        scratch_shapes=[pltpu.SemaphoreType.DMA],
        cost_estimate=pl.CostEstimate(flops=0, bytes_accessed=2 * shape[0] * shape[1], transcendentals=0),
        compiler_params=pltpu.CompilerParams(vmem_limit_bytes=1 << 20),
        name="fetch",
    )(afar(array))


def feed_forward(front, back, shared_gate, shared_down, gates, shared_up, expert_gate, expert_up, expert_down, bn):
    count = 2 * front.shape[0]
    width, units = expert_gate.shape
    shared_units = shared_gate.shape[1]
    bd = 512 if width % 512 == 0 else width
    assert units % bn == 0
    per_slot = max(q for q in range(1, width // bd + 1) if (width // bd) % q == 0 and (q == 1 or q * units <= width))
    slot_rows = max(width, per_slot * units)
    slots = 4
    half = count // 2
    weight_bytes = 2 * 3 * width * (units + shared_units)
    return pl.pallas_call(
        functools.partial(ffn_kernel, bn, bd, per_slot, slots, len(gates)),
        out_shape=(pltpu.VMEM((half, width), jnp.float32), pltpu.VMEM((half, width), jnp.bfloat16)),
        in_specs=[VMEM, VMEM] + [VMEM] * (2 + len(gates)) + [HBM] * 4,
        out_specs=(VMEM, VMEM),
        scratch_shapes=[
            pltpu.VMEM((slots, slot_rows, max(bn, bd)), jnp.bfloat16),
            pltpu.VMEM(shared_up.shape, jnp.bfloat16),
            pltpu.VMEM((count, max(1, len(gates)) * bn), jnp.float32),
            pltpu.VMEM((count, width), jnp.bfloat16),
            pltpu.VMEM((count, width), jnp.bfloat16),
            pltpu.VMEM((count, units), jnp.bfloat16),
            pltpu.VMEM((count, shared_units), jnp.bfloat16),
            pltpu.SemaphoreType.DMA((slots, per_slot)),
            pltpu.SemaphoreType.DMA,
        ],
        cost_estimate=pl.CostEstimate(flops=count * weight_bytes, bytes_accessed=weight_bytes, transcendentals=0),
        compiler_params=pltpu.CompilerParams(vmem_limit_bytes=28 << 20),
        name="feed_forward",
    )(front, back, nearby(shared_gate), nearby(shared_down), *map(nearby, gates),
      *map(afar, (shared_up, expert_gate, expert_up, expert_down)))


def per_device(
    steps,
    fetches,
    query_rows,
    cache_keys,
    cache_values,
    residual,
    lengths,
    expert_ids,
    capacity,
    norm_gain,
    router,
    shared_gate,
    shared_up,
    shared_down,
    expert_gate,
    expert_up,
    expert_down,
):
    toks = query_rows.shape[1]
    units = expert_gate.shape[1]
    bn = min(512, units)
    row, stream, near_gate = attend_rows(
        query_rows[0], cache_keys[0], cache_values[0], residual[0], lengths[0],
        expert_ids[0].reshape(toks), capacity, norm_gain, router, shared_gate,
    )
    wanted = [(shared_down,)] + [(expert_gate, i * bn, bn) for i in range(units // bn)]
    near = []
    for i in range(min(fetches, len(wanted))):
        near.append(fetch(*wanted[i]))
    rows = row
    for i, (axis, pairs) in enumerate(steps):
        other = lax.ppermute(rows, axis, pairs)
        if i < len(steps) - 1:
            rows = jnp.concatenate([rows, other], axis=0)
    keep, send = feed_forward(
        rows, other, near_gate, near[0], near[1:],
        shared_up, expert_gate, expert_up, expert_down, bn,
    )
    back = list(reversed(steps))
    i = 0
    while i < len(back):
        if i and i + 1 < len(back):
            (axis, first), (_, second) = back[i], back[i + 1]
            both = tuple((src, second[dst][1]) for src, dst in first)
            size = keep.shape[0]
            total = keep
            for part, pairs in enumerate((second, first, both)):
                piece = send[part * size:(part + 1) * size]
                total = total + lax.ppermute(piece, axis, pairs).astype(jnp.float32)
            i += 2
        else:
            total = keep + lax.ppermute(send, *back[i]).astype(jnp.float32)
            i += 1
        rows_left = total.shape[0]
        share = rows_left // 4 if i + 1 < len(back) else rows_left // 2
        keep, send = total[:share], total[share:].astype(jnp.bfloat16)
    return (stream + total).astype(jnp.bfloat16)[None]


def exchange_steps(mesh):
    steps = []
    for axis in ("grp", "sub"):
        size = mesh.shape[axis]
        assert size & (size - 1) == 0
        bit = size >> 1
        while bit:
            steps.append((axis, tuple((i, i ^ bit) for i in range(size))))
            bit >>= 1
    return tuple(steps)


def solution(mesh):
    placed = (
        P(("grp", "sub"), "rep", None),
        P(("grp", "sub"), "rep", None, None),
        P(("grp", "sub"), "rep", None, None),
        P(("grp", "sub"), "rep", None),
        P(("grp", "sub"), "rep"),
        P(("grp", "sub"), "rep", None),
        P(),
        P(),
        P(),
        P(None, ("grp", "sub")),
        P(None, ("grp", "sub")),
        P(("grp", "sub"), None),
        P(None, ("grp", "sub")),
        P(None, ("grp", "sub")),
        P(("grp", "sub"), None),
    )
    steps = exchange_steps(mesh)
    fetches = min(FETCHES, len(steps))
    return jax.shard_map(
        functools.partial(per_device, steps, fetches),
        mesh=mesh,
        in_specs=placed,
        out_specs=P(("grp", "sub"), "rep", None),
        check_vma=False,
    )
```
